32 devices in a mesh: fsdp: 8 (over y, x, core), cp: 4 (over z).
Axes of the slice: x: 2, y: 2, z: 4, core: 2. Of those that a mesh axis runs over, the one named last changes fastest.
Arguments:
- features: bfloat16 [8, 512, 2560], P('fsdp', 'cp'), may hold values from -6 to 6
- query_rows: bfloat16 [8, 512, 1280], P('fsdp', 'cp'), may hold values from -40 to 40, as said below
- key_rows: bfloat16 [8, 512, 1280], P('fsdp', 'cp'), may hold values from -4 to 4
- value_rows: bfloat16 [8, 512, 1280], P('fsdp', 'cp'), may hold values from -6 to 6
- attn_output: bfloat16 [8, 512, 1280], P('fsdp', 'cp'), may hold values from -6 to 6
- grad_output: bfloat16 [8, 512, 1280], P('fsdp', 'cp'), may hold values from -6 to 6
- log_sums: float32 [8, 512, 10], P('fsdp', 'cp'), as said below
Outputs:
- d_query: bfloat16 [8, 512, 1280], P('fsdp', 'cp')
- d_key: bfloat16 [8, 512, 1280], P('fsdp', 'cp')
- d_value: bfloat16 [8, 512, 1280], P('fsdp', 'cp')
- d_value_weight: float32 [2560, 1280], P('fsdp', 'cp')
The draws below stay inside these ranges and needn't reach their ends.
Inputs may be any that keep to these rules, and one draw needn't show every extreme that they name: `query_rows`: queries of a clip, with key_rows and log_sums drawn together with them. log_sums[c, t, h] is the logarithm of the sum over all 512 keys u of clip c of exp(128**-0.5 * q[t] . k[u]) for head h, computed from the bfloat16 queries and keys in float32.
All inputs are finite; a program needn't handle non-finite values.
Results may differ from the reference program's by a relative error of at most 0.02.
Values may be sent and summed in bfloat16 or wider, within the bound.
No kernel may reach another device: no remote copies, remote signals or barrier semaphores. Data moves between devices by JAX's collectives and lax.ppermute only.
A program may use at most 128 MiB of HBM per device.

```python
import jax
import jax.numpy as jnp
from jax import lax

D = 2560
HEADS = 10
HEAD = 128
TOK_DEV = 128
CLIPS = 8
SEQ = 512
QKV_WIDTH = 1280
N_CP = 4


def pair_draw(key):
    query_key = jax.random.fold_in(key, 101)
    key_key = jax.random.fold_in(key, 202)
    full_shape = (CLIPS, SEQ, HEADS * HEAD)
    key_vals = jax.random.truncated_normal(key_key, -4.0, 4.0, full_shape, jnp.float32)
    query_vals = jax.random.truncated_normal(query_key, -4.0, 4.0, full_shape, jnp.float32)
    query_half = query_vals.astype(jnp.bfloat16)
    key_half = key_vals.astype(jnp.bfloat16)
    query_side = query_half.astype(jnp.float32)
    key_side = key_half.astype(jnp.float32)

    def clip_norms(operands):
        query_heads = operands[0].reshape(SEQ, HEADS, HEAD)
        key_heads = operands[1].reshape(SEQ, HEADS, HEAD)
        scores = jnp.einsum('qhd,khd->hqk', query_heads, key_heads, precision=lax.Precision.HIGHEST) * HEAD ** (-0.5)
        return jax.nn.logsumexp(scores, axis=2).T
    log_norms = lax.map(clip_norms, (query_side, key_side)).astype(jnp.float32)
    return (query_half, key_half, log_norms)


def draw_query_rows(key, part):
    return pair_draw(key)[0]


def draw_key_rows(key, part):
    return pair_draw(key)[1]


def draw_log_sums(key, part):
    return pair_draw(key)[2]


def strengthened(drawn, own_key, source, target, parts, factor):
    def block_of(position):
        return (jnp.arange(drawn.shape[position]) // (drawn.shape[position] // parts)).reshape((-1,) + (1,) * (drawn.ndim - 1 - position))

    first = jax.random.permutation(own_key, parts)[block_of(target)]
    other_side = (block_of(target) + parts // 2) % parts
    return jnp.where((block_of(source) == first) | (block_of(source) == other_side), factor * drawn, drawn)


def shard_levels(stream_key, dims, shards, smallest, top_value):
    def one(position, shards_of):
        heights = jax.random.uniform(jax.random.fold_in(jax.random.fold_in(stream_key, 6), position), (shards_of,), jnp.float32, smallest / len(shards), top_value / len(shards))
        return jnp.repeat(jnp.exp(heights), dims[position] // shards_of).reshape((-1,) + (1,) * (len(dims) - position - 1))

    loudness = one(*shards[0])
    for cut in shards[1:]:
        loudness = loudness * one(*cut)
    return loudness


def normal_values(key, shape, width, limit, pieces=(), dtype=jnp.bfloat16):
    values = width * jax.random.normal(key, shape, jnp.float32)
    if pieces:
        values = values * shard_levels(key, shape, pieces, -0.22, 0.18)
    return jnp.clip(values, -limit, limit).astype(dtype)


def noise_with(rng, extent, deviation, most, pieces, heavy, dtype=jnp.bfloat16):
    values = deviation * jax.random.normal(rng, extent, jnp.float32)
    if pieces:
        values = values * shard_levels(rng, extent, pieces, -0.22, 0.18)
    return jnp.clip(strengthened(values, jax.random.fold_in(rng, 3), *heavy), -most, most).astype(dtype)


def setup_inputs(seed: int = 0) -> dict:
    seeds = jax.random.split(jax.random.key(seed), 8)
    features = noise_with(seeds[0], (CLIPS, SEQ, D), 1.0, 6.0, ((0, 8), (1, 4)), (0, 2, 8, 2.0))
    query_rows = draw_query_rows(jax.random.fold_in(seeds[7], 71), 0)
    key_rows = draw_key_rows(jax.random.fold_in(seeds[7], 71), 0)
    value_rows = normal_values(seeds[3], (CLIPS, SEQ, QKV_WIDTH), 1.0, 6.0, ((0, 8), (1, 4)))
    attn_output = normal_values(seeds[4], (CLIPS, SEQ, QKV_WIDTH), 1.0, 6.0, ((0, 8), (1, 4)))
    grad_output = normal_values(seeds[5], (CLIPS, SEQ, QKV_WIDTH), 1.0, 6.0, ((0, 8), (1, 4)))
    log_sums = draw_log_sums(jax.random.fold_in(seeds[7], 71), 0)
    return {"features": features, "query_rows": query_rows, "key_rows": key_rows, "value_rows": value_rows, "attn_output": attn_output, "grad_output": grad_output, "log_sums": log_sums}


def split_heads(matrix):
    return matrix.reshape(matrix.shape[0], HEADS, HEAD).astype(jnp.float32)


def clip_backward(operands):
    queries, key_side, value_side, attn_out, grad_out, log_norm, inputs = operands
    softmax_scale = HEAD ** -0.5
    query_heads = split_heads(queries)
    key_heads = split_heads(key_side)
    value_heads = split_heads(value_side)
    grad_heads = split_heads(grad_out)
    row_delta = jnp.sum(grad_heads * split_heads(attn_out), axis=2)
    scores = jnp.einsum("qhd,khd->hqk", query_heads, key_heads) * softmax_scale
    attn_prob = jnp.exp(scores - log_norm.T[:, :, None])
    grad_prob = jnp.einsum("qhd,khd->hqk", grad_heads, value_heads)
    grad_score = (attn_prob * (grad_prob - row_delta.T[:, :, None])).astype(jnp.bfloat16)
    grad_score = lax.optimization_barrier(grad_score).astype(jnp.float32)
    grad_query = softmax_scale * jnp.einsum("hqk,khd->qhd", grad_score, key_heads)
    grad_key = softmax_scale * jnp.einsum("hqk,qhd->khd", grad_score, query_heads)
    prob_rounded = lax.optimization_barrier(attn_prob.astype(jnp.bfloat16)).astype(jnp.float32)
    grad_value = jnp.einsum("hqk,qhd->khd", prob_rounded, grad_heads)
    grad_query = grad_query.reshape(SEQ, QKV_WIDTH).astype(jnp.bfloat16)
    grad_key = grad_key.reshape(SEQ, QKV_WIDTH).astype(jnp.bfloat16)
    grad_value = grad_value.reshape(SEQ, QKV_WIDTH).astype(jnp.bfloat16)
    feature_blocks = inputs.reshape(N_CP, TOK_DEV, D)
    value_blocks = grad_value.reshape(N_CP, TOK_DEV, QKV_WIDTH)

    def add_block(running, blocks):
        block_term = jnp.dot(blocks[0].T, blocks[1], preferred_element_type=jnp.float32)
        rounded = lax.optimization_barrier(block_term.astype(jnp.bfloat16)).astype(jnp.float32)
        return running + rounded, None

    weight_sum, _ = lax.scan(add_block, jnp.zeros((D, QKV_WIDTH), jnp.float32), (feature_blocks, value_blocks))
    return grad_query, grad_key, grad_value, weight_sum


def reference(features, query_rows, key_rows, value_rows, attn_output, grad_output, log_sums):
    results = lax.map(clip_backward, (query_rows, key_rows, value_rows, attn_output, grad_output, log_sums, features))
    return results[0], results[1], results[2], jnp.sum(results[3], axis=0)
```

```python
import functools
import math

import jax
import jax.numpy as jnp
from jax import lax
from jax.experimental import pallas as pl
from jax.experimental.pallas import tpu as pltpu
from jax.sharding import PartitionSpec as P

F32 = jnp.float32
BF16 = jnp.bfloat16
PARTS = 6


def three_parts(row):
    high = row.astype(BF16).astype(F32)
    rest = row - high
    mid = rest.astype(BF16).astype(F32)
    return high, mid, rest - mid


def extra_rows(count):
    return -(-count * PARTS // 16) * 16


def head_groups(per_pos, groups):
    if groups != 2 or per_pos < 3:
        return [list(range(per_pos))]
    first = [h for h in range(per_pos) if h % 2 == 0 or per_pos % 2 == 0 and h in (0, per_pos - 1)]
    first = sorted(set(first) | {per_pos - 1 - h for h in first})
    second = [h for h in range(per_pos) if h not in first]
    return [first, second] if second else [first]


def column_runs(chunks, per_pos, groups, head_size):
    width = per_pos * head_size // groups
    runs = []
    for owner in range(groups):
        found = []
        for index, heads in enumerate(chunks):
            piece = len(heads) * head_size // groups
            unit = math.gcd(piece, head_size)
            for start in range(0, piece, unit):
                at = owner * piece + start
                column = heads[at // head_size] * head_size + at % head_size
                found.append((column - owner * width, index, start, unit))
        found.sort()
        place = 0
        for column, _, _, unit in found:
            assert column == place
            place += unit
        assert place == width
        runs.append([(index, start, unit) for _, index, start, unit in found])
    return runs


def pack_kernel(dims, heads, q_ref, k_ref, v_ref, o_ref, g_ref, norm_ref, *outs):
    members, groups, per_pos, tokens, size = dims
    pos = lax.rem(lax.axis_index("cp"), members)
    extra = extra_rows(len(heads))
    ones = jnp.ones((8, size), BF16)
    row_id = lax.broadcasted_iota(jnp.int32, (extra, tokens), 0)
    for b in range(members):
        owner = lax.rem(pos + b, members)
        full = outs[b]
        side = jnp.zeros((extra, tokens), F32)
        for i, head in enumerate(heads):
            number = owner * per_pos + head
            lanes = pl.ds(pl.multiple_of(number * size, size), size)
            grad = g_ref[:, lanes]
            product = grad.astype(F32) * o_ref[:, lanes].astype(F32)
            high = product.astype(BF16)
            low = (product - high.astype(F32)).astype(BF16)
            contract = (((1,), (1,)), ((), ()))
            delta = lax.dot_general(ones, high, contract, preferred_element_type=F32)
            delta += lax.dot_general(ones, low, contract, preferred_element_type=F32)
            norm = norm_ref[pl.ds(number, 1), :]
            values = three_parts(norm) + three_parts(delta[0:1, :])
            for part, value in enumerate(values):
                side = jnp.where(row_id == i * PARTS + part, value, side)
            at = 2 * i * tokens
            query = q_ref[:, lanes]
            base = 2 * len(heads) * tokens + extra + at
            full[at : at + tokens, :] = query
            full[at + tokens : at + 2 * tokens, :] = grad
            full[base : base + tokens, :] = k_ref[:, lanes]
            full[base + tokens : base + 2 * tokens, :] = v_ref[:, lanes]
            if groups > 1:
                outs[members + b][at : at + tokens, :] = query
                outs[members + b][at + tokens : at + 2 * tokens, :] = grad
        at = 2 * len(heads) * tokens
        side = side.astype(BF16)
        full[at : at + extra, :] = side
        if groups > 1:
            outs[members + b][at : at + extra, :] = side


def attn_kernel(dims, count, *refs):
    members, groups, _, tokens, size = dims
    sources = members * groups
    blocks = refs[:sources]
    grad_value, returns = refs[sources], refs[sources + 1 :]
    scale = size ** (-0.5)
    extra = extra_rows(count)
    side_at = 2 * count * tokens
    sides = [block[side_at : side_at + extra, :].astype(F32) for block in blocks]
    rows_rows = (((1,), (1,)), ((), ()))

    def side_row(first):
        return jnp.concatenate(
            [s[first : first + 1] + s[first + 1 : first + 2] + s[first + 2 : first + 3] for s in sides],
            axis=1,
        )

    for i in range(count):
        at = 2 * i * tokens
        kv_at = side_at + extra + at
        lanes = slice(i * size, (i + 1) * size)
        keys = jnp.concatenate([blocks[b][kv_at : kv_at + tokens, :] for b in range(members)], axis=0)
        values = jnp.concatenate(
            [blocks[b][kv_at + tokens : kv_at + 2 * tokens, :] for b in range(members)], axis=0
        )
        queries = jnp.concatenate([block[at : at + tokens, :] for block in blocks], axis=0)
        grads = jnp.concatenate([block[at + tokens : at + 2 * tokens, :] for block in blocks], axis=0)
        scores = lax.dot_general(keys, queries, rows_rows, preferred_element_type=F32)
        prob = jnp.exp(scores * scale - side_row(i * PARTS))
        grad_v = jnp.dot(prob.astype(BF16), grads, preferred_element_type=F32).astype(BF16)
        grad_value[:, lanes] = grad_v
        grad_prob = lax.dot_general(values, grads, rows_rows, preferred_element_type=F32)
        grad_score = (prob * (grad_prob - side_row(i * PARTS + 3))).astype(BF16)
        grad_k = (scale * jnp.dot(grad_score, queries, preferred_element_type=F32)).astype(BF16)
        grad_q = lax.dot_general(
            grad_score, keys, (((0,), (0,)), ((), ())), preferred_element_type=F32
        )
        grad_q = (scale * grad_q).astype(BF16)
        for source in range(sources):
            rows = slice(source * tokens, (source + 1) * tokens)
            returns[source][:, lanes] = grad_q[rows]
            if source < members:
                second = slice((count + i) * size, (count + i + 1) * size)
                third = slice((2 * count + i) * size, (2 * count + i + 1) * size)
                returns[source][:, second] = grad_k[rows]
                returns[source][:, third] = grad_v[rows]


def finish_kernel(dims, chunks, *refs):
    members, groups, per_pos, _, size = dims
    sources = members * groups
    pos = lax.rem(lax.axis_index("cp"), members)
    returned = refs[: sources * len(chunks)]
    d_query, d_key, d_value = refs[sources * len(chunks) :]
    for b in range(members):
        owner = lax.rem(pos + b, members)
        for index, heads in enumerate(chunks):
            mine = returned[index * sources : (index + 1) * sources]
            for i, head in enumerate(heads):
                lanes = pl.ds(pl.multiple_of((owner * per_pos + head) * size, size), size)
                part = slice(i * size, (i + 1) * size)
                total = mine[b][:, part].astype(F32)
                for a in range(1, groups):
                    total += mine[a * members + b][:, part].astype(F32)
                d_query[:, lanes] = total.astype(BF16)
                count = len(heads)
                d_key[:, lanes] = mine[b][:, (count + i) * size : (count + i + 1) * size]
                d_value[:, lanes] = mine[b][:, (2 * count + i) * size : (2 * count + i + 1) * size]


def weight_kernel(chips, cores, *refs):
    features, grads = refs[:chips], refs[chips : 2 * chips]
    outs, total = refs[2 * chips : 2 * chips + cores], refs[-1]
    sums = None
    for x, g in zip(features, grads):
        term = lax.dot_general(x[...], g[...], (((0,), (0,)), ((), ())), preferred_element_type=F32)
        sums = term if sums is None else sums + term
    total[...] = sums
    core = lax.rem(lax.axis_index("fsdp"), cores)
    rows = outs[0].shape[0]
    for c, out in enumerate(outs):
        at = pl.multiple_of(lax.rem(core + c, cores) * rows, 16)
        out[...] = total[pl.ds(at, rows), :].astype(out.dtype)


def call(kernel, shapes, args, flops=0, exps=0, scratch=()):
    moved = sum(a.size * a.dtype.itemsize for a in args) + sum(
        math.prod(s.shape) * s.dtype.itemsize for s in shapes
    )
    return pl.pallas_call(
        kernel,
        out_shape=tuple(shapes),
        in_specs=[pl.BlockSpec(memory_space=pltpu.VMEM)] * len(args),
        out_specs=tuple(pl.BlockSpec(memory_space=pltpu.VMEM) for _ in shapes),
        scratch_shapes=scratch,
        cost_estimate=pl.CostEstimate(flops=flops, bytes_accessed=moved, transcendentals=exps),
    )(*args)


def on_device(features, query_rows, key_rows, value_rows, attn_output, grad_output, log_sums):
    tokens, width = query_rows.shape[1:]
    total_heads = log_sums.shape[2]
    size = width // total_heads
    spread, fleet = lax.axis_size("cp"), lax.axis_size("fsdp")
    members = math.gcd(spread, total_heads)
    groups = spread // members
    per_pos = total_heads // members
    cores = 2 if fleet % 2 == 0 else 1
    chips = fleet // cores
    dims = (members, groups, per_pos, tokens, size)
    chunks = head_groups(per_pos, groups)
    owned = column_runs(chunks, per_pos, groups, size)
    place = lax.axis_index("cp")
    group, pos = place // members, place % members
    unit = lax.axis_index("fsdp")

    def peer(index, a, b):
        return (index // members + a) % groups * members + (index % members + b) % members

    def send(value, a, b):
        return lax.ppermute(value, "cp", [(i, peer(i, a, b)) for i in range(spread)])

    def send_back(value, a, b):
        return lax.ppermute(value, "cp", [(peer(i, a, b), i) for i in range(spread)])

    def other_chip(chip, k):
        return chip ^ k if chips & (chips - 1) == 0 else (chip + k) % chips

    def to_chip(value, k):
        pairs = [(i, other_chip(i // cores, k) * cores + i % cores) for i in range(fleet)]
        return lax.ppermute(value, "fsdp", pairs)

    shifts = [(a, b) for a in range(groups) for b in range(members)]
    flat = [v[0] for v in (query_rows, key_rows, value_rows, attn_output, grad_output)]
    norms = log_sums[0].T

    arrived = []
    for heads in chunks:
        short = 2 * len(heads) * tokens + extra_rows(len(heads))
        long = short + 2 * len(heads) * tokens
        shapes = [jax.ShapeDtypeStruct((long, size), BF16)] * members
        if groups > 1:
            shapes += [jax.ShapeDtypeStruct((short, size), BF16)] * members
        packed = call(functools.partial(pack_kernel, dims, heads), shapes, (*flat, norms))
        blocks = [packed[0]]
        for a, b in shifts[1:]:
            blocks.append(send(packed[b if a == 0 else members + b], a, b))
        arrived.append(blocks)

    pieces = [features[0]] + [send(features, 0, b)[0] for b in range(1, members)]
    chip_rows = features.shape[2] // chips
    columns = []
    for k in range(chips):
        start = other_chip(unit // cores, k) * chip_rows
        block = jnp.concatenate(
            [lax.dynamic_slice_in_dim(p, start, chip_rows, 1) for p in pieces], axis=0
        )
        columns.append(block if k == 0 else to_chip(block, k))

    returned, weight_parts = [], []
    for heads, blocks in zip(chunks, arrived):
        count = len(heads)
        shapes = [jax.ShapeDtypeStruct((members * tokens, count * size), BF16)]
        for a, b in shifts:
            shapes.append(jax.ShapeDtypeStruct((tokens, (3 if a == 0 else 1) * count * size), BF16))
        area = members * tokens * spread * tokens * count
        grad_value, *back = call(
            functools.partial(attn_kernel, dims, count), shapes, blocks, 10 * area * size, area
        )
        gathered = [grad_value] + [to_chip(grad_value, k) for k in range(1, chips)]
        returned.append(back[:1] + [send_back(r, a, b) for r, (a, b) in zip(back[1:], shifts[1:])])

        rows = chip_rows // cores
        shapes = [jax.ShapeDtypeStruct((rows, count * size), F32)]
        shapes += [jax.ShapeDtypeStruct((rows, count * size), BF16)] * (cores - 1)
        own, *others = call(
            functools.partial(weight_kernel, chips, cores),
            shapes,
            (*columns, *gathered),
            2 * chip_rows * count * size * chips * members * tokens,
            scratch=[pltpu.VMEM((chip_rows, count * size), F32)],
        )
        for c, other in enumerate(others, 1):
            pairs = [(i, i // cores * cores + (i + c) % cores) for i in range(fleet)]
            own = own + lax.ppermute(other, "fsdp", pairs).astype(F32)
        piece = count * size // groups
        total = None
        for r in range(groups):
            block = lax.dynamic_slice_in_dim(own, (group + r) % groups * piece, piece, 1).astype(BF16)
            pairs = [
                (g * members + p, p * groups + (g + r) % groups)
                for g in range(groups)
                for p in range(members)
            ]
            block = lax.ppermute(block, "cp", pairs).astype(F32)
            total = block if total is None else total + block
        weight_parts.append(total)

    shapes = [jax.ShapeDtypeStruct((tokens, width), BF16)] * 3
    d_query, d_key, d_value = call(
        functools.partial(finish_kernel, dims, chunks), shapes, [r for back in returned for r in back]
    )

    def assembled(owner):
        return jnp.concatenate(
            [weight_parts[i][:, s : s + n] for i, s, n in owned[owner]], axis=1
        )

    weight = assembled(0)
    for owner in range(1, groups):
        if owned[owner] != owned[0]:
            weight = jnp.where(place % groups == owner, assembled(owner), weight)
    return (d_query[None], d_key[None], d_value[None], weight)


def solution(mesh):
    tokens = P("fsdp", "cp", None)
    return jax.shard_map(
        on_device,
        mesh=mesh,
        in_specs=(tokens,) * 7,
        out_specs=(tokens, tokens, tokens, P("fsdp", "cp")),
        check_vma=False,
    )
```
